128 devices in a mesh: row: 4 (over y_lo, core), col: 32 (over z, y_hi, x).
Axes of the slice: x: 4, y: 4 (y_hi: 2, y_lo: 2; y = y_hi * 2 + y_lo), z: 4, core: 2. Of those that a mesh axis runs over, the one named last changes fastest.
Arguments:
- orbitals: bfloat16 [256, 8, 48, 2304], P(('row', 'col')), may hold values from -6 to 6
- potential_boxes: float32 [256, 48, 2304], P(('row', 'col')), may hold values from 0 to 2
- corners: int32 [256, 3], P(('row', 'col')), may hold values from 0 to 511, as said below
- signs: int32 [256], P(('row', 'col')), may hold values from -1 to 1, as said below
- counts: int32 [256], P(('row', 'col')), may hold values from 1 to 8, as said below
Outputs:
- filtered: bfloat16 [256, 8, 48, 2304], P(('row', 'col'))
- density: float32 [64, 256, 512], P('row', 'col')
- hartree: float32 [64, 256, 512], P('row', 'col')
The draws below stay inside these ranges and needn't reach their ends.
Inputs may be any that keep to these rules, and one draw needn't show every extreme that they name: `corners`: for fragment f held at index d = f // 2 of the row+col axis, with r = d // 32 and c = d % 32, the corner's first entry lies in [r * 16, (r + 1) * 16) and its second in [c * 8, (c + 1) * 8); the third is any cell below 512. Fragments 2 i and 2 i + 1 have the same corner. Each entry is -1 or 1; fragments 2 i and 2 i + 1 have opposite signs. Fragments 2 i and 2 i + 1 have equal counts; some device holds a fragment with 8 and some device one with 1.
All inputs are finite; a program needn't handle non-finite values.
Results may differ from the reference program's by a relative error of at most 0.001.
Values may be sent and summed in bfloat16 or wider, within the bound.
No kernel may reach another device: no remote copies, remote signals or barrier semaphores. Data moves between devices by JAX's collectives and lax.ppermute only.
A program may use at most 128 MiB of HBM per device.

```python
import math
import jax
import jax.numpy as jnp
from jax import lax

B = 48
ORB = 8
DEGREE = 6
FRAG_DEV = 2
CX = 16
CY = 8
NZ = 512
FRAGS = 256
NX = 64
NY = 256


def draw_corners(key, part):
    columns = NY // CY
    pairs = FRAGS // 2
    owner = 2 * jnp.arange(pairs, dtype=jnp.int32) // FRAG_DEV
    keys = jax.random.split(jax.random.fold_in(key, 11), 3)
    xs = owner // columns * CX + jax.random.randint(keys[0], (pairs,), 0, CX)
    ys = owner % columns * CY + jax.random.randint(keys[1], (pairs,), 0, CY)
    zs = jax.random.randint(keys[2], (pairs,), 0, NZ)
    paired = jnp.stack([xs, ys, zs], axis=1).astype(jnp.int32)
    return jnp.repeat(paired, 2, axis=0).astype(jnp.int32)


def draw_signs(key, part):
    pairs = FRAGS // 2
    first = 2 * jax.random.randint(jax.random.fold_in(key, 5), (pairs,), 0, 2) - 1
    return jnp.stack([first, -first], axis=1).reshape(FRAGS).astype(jnp.int32)


def draw_counts(key, part):
    holders = FRAGS // FRAG_DEV
    per_holder = FRAG_DEV // 2
    keys = jax.random.split(jax.random.fold_in(key, 23), 4)
    ceiling = jax.random.randint(keys[0], (holders, 1), 1, ORB + 1)
    spread = jax.random.randint(keys[1], (holders, per_holder), 0, ORB)
    pair_counts = 1 + spread % ceiling
    full_holder = jax.random.randint(keys[2], (), 0, holders)
    single_holder = (full_holder + 1 + jax.random.randint(keys[3], (), 0, holders - 1)) % holders
    holder_rows = jnp.arange(holders, dtype=jnp.int32)[:, None]
    first_pair = (jnp.arange(per_holder, dtype=jnp.int32) == 0)[None, :]
    pair_counts = jnp.where((holder_rows == full_holder) & first_pair, ORB, pair_counts)
    pair_counts = jnp.where((holder_rows == single_holder) & first_pair, 1, pair_counts)
    return jnp.repeat(pair_counts.reshape(holders * per_holder), 2).astype(jnp.int32)


def draw_orbitals(key, part):
    field = jax.random.normal(jax.random.fold_in(key, 37), (FRAGS, ORB, B, B * B), jnp.float32)
    return jnp.clip(field, -6.0, 6.0).astype(jnp.bfloat16)


def draw_potential_boxes(key, part):
    return jax.random.uniform(jax.random.fold_in(key, 43), (FRAGS, B, B * B), jnp.float32, 0.0, 2.0)


def setup_inputs(seed: int = 0) -> dict:
    key_of = jax.random.split(jax.random.key(seed), 6)
    orbitals = draw_orbitals(jax.random.fold_in(key_of[5], 71), 0)
    potential_boxes = draw_potential_boxes(jax.random.fold_in(key_of[5], 71), 0)
    corners = draw_corners(jax.random.fold_in(key_of[5], 71), 0)
    signs = draw_signs(jax.random.fold_in(key_of[5], 71), 0)
    counts = draw_counts(jax.random.fold_in(key_of[5], 71), 0)
    return dict(orbitals=orbitals, potential_boxes=potential_boxes, corners=corners, signs=signs, counts=counts)


CENTER = 5.25
HALF_WIDTH = 3.75
SCREEN = 0.0025

def hamiltonian(field, potential):
    side = field.shape[0]
    zpos = lax.broadcasted_iota(jnp.int32, field.shape, 1) % side
    zero_row = jnp.zeros_like(field[:1])
    next_x = jnp.concatenate([field[1:], zero_row], 0)
    prev_x = jnp.concatenate([zero_row, field[:-1]], 0)
    zero_col = jnp.zeros_like(field[:, :1])
    next_z = jnp.concatenate([field[:, 1:], zero_col], 1)
    prev_z = jnp.concatenate([zero_col, field[:, :-1]], 1)
    next_z = jnp.where(zpos == side - 1, 0.0, next_z)
    prev_z = jnp.where(zpos == 0, 0.0, prev_z)
    zero_plane = jnp.zeros_like(field[:, :side])
    next_y = jnp.concatenate([field[:, side:], zero_plane], 1)
    prev_y = jnp.concatenate([zero_plane, field[:, :-side]], 1)
    beside = next_x + prev_x + next_z + prev_z + next_y + prev_y
    return (3.0 + potential) * field - 0.5 * beside

def chebyshev(start, potential):

    def shifted(field):
        return (hamiltonian(field, potential) - CENTER * field) / HALF_WIDTH
    previous = start
    current = shifted(start)
    for order in range(2, DEGREE + 1):
        previous, current = (current, 2.0 * shifted(current) - previous)
    scale = lax.rsqrt(jnp.mean(current * current) + 1e-06)
    return current * scale

def wave_square(length, positions):
    signed_index = jnp.where(positions <= length // 2, positions, positions - length).astype(jnp.float32)
    wave = signed_index * (2 * math.pi / length)
    return wave * wave

def one_fragment(items):
    orbital_set, potential, live_count = items
    result = jax.vmap(lambda single: chebyshev(single.astype(jnp.float32), potential))(orbital_set)
    live = (jnp.arange(ORB, dtype=jnp.int32) < live_count)[:, None, None]
    result = jnp.where(live, result, 0.0)
    return (result.astype(jnp.bfloat16), lax.optimization_barrier(jnp.sum(result * result, axis=0)))

def reference(orbitals, potential_boxes, corners, signs, counts):
    filtered, boxes = lax.map(one_fragment, (orbitals, potential_boxes, counts))
    signed = boxes * signs.astype(jnp.float32)[:, None, None]
    cubes = signed.reshape(FRAGS, B, B, B)
    padded = jnp.zeros((NX + B, NY + B, NZ + B), jnp.float32)

    def place(grid, item):
        cube, corner = item
        start = (corner[0], corner[1], corner[2])
        region = lax.dynamic_slice(grid, start, (B, B, B))
        return (lax.dynamic_update_slice(grid, region + cube, start), None)
    padded, _ = lax.scan(place, padded, (cubes, corners))
    grid = padded[:NX].at[:B].add(padded[NX:])
    grid = grid[:, :NY].at[:, :B].add(grid[:, NY:])
    density = grid[:, :, :NZ].at[:, :, :B].add(grid[:, :, NZ:])
    spectrum = jnp.fft.fftn(density)
    k_square = wave_square(NX, jnp.arange(NX, dtype=jnp.int32))[:, None, None] + wave_square(NY, jnp.arange(NY, dtype=jnp.int32))[None, :, None] + wave_square(NZ, jnp.arange(NZ, dtype=jnp.int32))[None, None, :]
    factor = jnp.where(k_square > 0, SCREEN / (k_square + SCREEN), 0.0)
    hartree = jnp.real(jnp.fft.ifftn(spectrum * factor)).astype(jnp.float32)
    return (filtered, density, hartree)
```

```python
import math

import jax
import jax.numpy as jnp
import numpy as np
from jax import lax
from jax.experimental import pallas as pl
from jax.experimental.pallas import tpu as pltpu
from jax.sharding import PartitionSpec as P

B = 48
YZ = B * B
TILES = YZ // 128
ORB = 8
LANES = 128
NX, NY, NZ = 64, 256, 512
CX, CY = 16, 8
SCREEN = 0.0025
BOTH = ("row", "col")
F32 = jnp.float32
BF16 = jnp.bfloat16

ROOTS = [7.5 * math.cos(math.pi * k / 12) for k in (1, 11, 5, 9, 3, 7)]
KAPPA = 32.0 / 7.5**6
PIECE = 56
NT = (((1,), (1,)), ((), ()))
NN = (((1,), (0,)), ((), ()))


def dot(a, b, dims=NN):
    return lax.dot_general(a, b, dims, preferred_element_type=F32)


def split(v):
    high = v.astype(BF16)
    return high, (v - high.astype(F32)).astype(BF16)


def dot_left(tab_h, tab_l, v, dims=NN):
    h, l = split(v)
    return dot(tab_h, h, dims) + (dot(tab_h, l, dims) + dot(tab_l, h, dims))


def dot_right(v, tab_h, tab_l, dims=NN):
    h, l = split(v)
    return dot(h, tab_h, dims) + (dot(l, tab_h, dims) + dot(h, tab_l, dims))


def cheb_kernel(meta, orb, pot, eye, sel, filt, send, buf_a, buf_b, diag, stage, box):
    lane = lax.broadcasted_iota(jnp.int32, (8, LANES), 1)
    sub = lax.broadcasted_iota(jnp.int32, (8, LANES), 0)
    first_x = lane % 8 == 0
    last_x = lane % 8 == 7
    zero = jnp.zeros((8, LANES), F32)
    for buf in (buf_a, buf_b):
        for xi in range(6):
            for k in range(6):
                buf[xi, 8 * k : 8 * k + 8, :] = zero
                buf[xi, 48 + YZ + 8 * k : 56 + YZ + 8 * k, :] = zero

    @pl.loop(0, TILES)
    def _(t):
        cols = pl.ds(pl.multiple_of(t * LANES, LANES), LANES)
        for f in range(2):
            stage[f * B : (f + 1) * B, :] = 4.5 - 2.0 * pot[f, :, cols]
        for xi in range(6):
            halves = [stage[pl.ds(f * B + xi, 8, stride=6), :] for f in range(2)]
            block = jnp.concatenate([halves[0]] * 8 + [halves[1]] * 8, 0)
            diag[xi, pl.ds(pl.multiple_of(t * LANES, LANES), LANES), :] = block.T

    @pl.loop(0, TILES)
    def _(t):
        cols = pl.ds(pl.multiple_of(t * LANES, LANES), LANES)
        for fo in range(16):
            stage[fo * B : (fo + 1) * B, :] = orb[fo, :, cols].astype(F32)
        for xi in range(6):
            block = jnp.concatenate(
                [stage[pl.ds(fo * B + xi, 8, stride=6), :] for fo in range(16)], 0
            )
            out = dot(eye[...], block.astype(BF16), NT)
            buf_a[xi, pl.ds(pl.multiple_of(48 + t * LANES, 16), LANES), :] = out

    def apply(src, dst, root, acc):
        def row(y, acc):
            base = pl.multiple_of(48 + 48 * y, 16)
            dbase = pl.multiple_of(48 * y, 16)
            for zt in range(6):
                r = base + 8 * zt
                mid = [src[xi, pl.ds(r, 8), :] for xi in range(6)]
                low = jnp.where(first_x, 0.0, pltpu.roll(mid[5], 1, 1))
                high = jnp.where(last_x, 0.0, pltpu.roll(mid[0], LANES - 1, 1))
                for xi in range(6):
                    below = src[xi, pl.ds(r - 1, 8), :]
                    above = src[xi, pl.ds(r + 1, 8), :]
                    if zt == 0:
                        below = jnp.where(sub == 0, 0.0, below)
                    if zt == 5:
                        above = jnp.where(sub == 7, 0.0, above)
                    beside = (src[xi, pl.ds(r - 48, 8), :] + src[xi, pl.ds(r + 48, 8), :]) + (
                        below + above
                    )
                    left = mid[xi - 1] if xi > 0 else low
                    right = mid[xi + 1] if xi < 5 else high
                    beside = beside + (left + right)
                    d = diag[xi, pl.ds(dbase + 8 * zt, 8), :]
                    out = (d - root) * mid[xi] + beside
                    dst[xi, pl.ds(r, 8), :] = out
                    if acc is not None:
                        acc = acc + out * out
            return acc

        if acc is None:

            @pl.loop(0, B)
            def _(y):
                row(y, None)

            return None
        return lax.fori_loop(0, B, row, acc)

    apply(buf_a, buf_b, ROOTS[0], None)
    apply(buf_b, buf_a, ROOTS[1], None)
    apply(buf_a, buf_b, ROOTS[2], None)
    apply(buf_b, buf_a, ROOTS[3], None)
    apply(buf_a, buf_b, ROOTS[4], None)
    total = apply(buf_b, buf_a, ROOTS[5], zero)

    total = jnp.broadcast_to(jnp.sum(total, axis=0, keepdims=True), (8, LANES))
    for step in (1, 2, 4):
        other = jnp.where(
            lane & step == 0,
            pltpu.roll(total, LANES - step, 1),
            pltpu.roll(total, step, 1),
        )
        total = total + other
    scale = KAPPA * lax.rsqrt(total * (KAPPA * KAPPA / B**3) + 1e-6)
    second = lane >= 64
    count = jnp.where(second, meta[4], meta[3])
    sign = jnp.where(second, meta[6], meta[5]).astype(F32)
    scale = jnp.where((lane // 8) % 8 < count, scale, 0.0)
    weight = (scale * scale * sign)[:1, :]
    scale = scale[:1, :]

    @pl.loop(0, 26)
    def _(t):
        for k in range(10):
            box[t, 8 * k : 8 * k + 8, :] = zero

    @pl.loop(0, TILES)
    def _(t):
        cols = pl.ds(pl.multiple_of(t * LANES, LANES), LANES)
        for xi in range(6):
            field = buf_a[xi, pl.ds(pl.multiple_of(48 + t * LANES, 16), LANES), :]
            out = dot(eye[...], (field * scale).astype(BF16), NT)
            for fo in range(16):
                stage[pl.ds(fo * B + xi, 8, stride=6), :] = out[8 * fo : 8 * fo + 8, :]
            dh, dl = split(field * field * weight)
            dens = dot(sel[...], dh, NT) + dot(sel[...], dl, NT)
            box[t + 4, pl.ds(16 + xi, 8, stride=6), :] = dens
        for fo in range(16):
            filt[fo, :, cols] = stage[fo * B : (fo + 1) * B, :].astype(BF16)

    shift_x = meta[0]
    lanes_y = meta[1] * B
    whole = lanes_y // LANES
    rest = lanes_y % LANES
    keep = lane < LANES - rest
    zvec = jnp.full((8, LANES), meta[2], jnp.int32).astype(F32)
    for j in range(7):
        for i in range(4):
            send[j, i, 48:56, :] = zvec

    @pl.loop(0, 7)
    def _(j):
        for tt in range(3):
            t0 = 3 * j + tt - whole + 4
            for k in range(8):
                rows = pl.ds(16 + 8 * k - shift_x, 8)
                merged = jnp.where(keep, box[t0, rows, :], box[t0 - 1, rows, :])
                r0 = tt * 16 + (k % 2) * 8
                send[j, (k // 2 + meta[7]) % 4, r0 : r0 + 8, :] = pltpu.roll(merged, rest, 1)


def filter_and_box(meta, orbitals, potential, eye, sel):
    vm = pl.BlockSpec(memory_space=pltpu.VMEM)
    return pl.pallas_call(
        cheb_kernel,
        out_shape=(
            jax.ShapeDtypeStruct((16, B, YZ), BF16),
            jax.ShapeDtypeStruct((7, 4, PIECE, LANES), F32),
        ),
        in_specs=[pl.BlockSpec(memory_space=pltpu.SMEM), vm, vm, vm, vm],
        out_specs=(vm, vm),
        scratch_shapes=[
            pltpu.VMEM((6, YZ + 96, LANES), F32),
            pltpu.VMEM((6, YZ + 96, LANES), F32),
            pltpu.VMEM((6, YZ, LANES), F32),
            pltpu.VMEM((16 * B, LANES), F32),
            pltpu.VMEM((26, 80, LANES), F32),
        ],
        compiler_params=pltpu.CompilerParams(vmem_limit_bytes=60 * 1024 * 1024),
        name="cheb",
    )(meta, orbitals, potential, eye, sel)


def slot_of(lane):
    return (lane // 16) % 4


def patch_kernel(pieces, tab_h, tab_l, dens, out, grid):
    lane = lax.broadcasted_iota(jnp.int32, (8, LANES), 1)
    zero = jnp.zeros((8, LANES), F32)
    for a in range(4):
        for k in range(16):
            grid[a, 8 * k : 8 * k + 8, :] = zero
    for p in range(28):
        z0 = jnp.max(pieces[p, 48:56, :]).astype(jnp.int32)
        for y in range(8):
            tile, off = (B * y) // LANES, (B * y) % LANES
            for k in range(2):
                v = pieces[p, tile * 16 + 8 * k : tile * 16 + 8 * k + 8, :]
                if off + B > LANES:
                    w = pieces[p, tile * 16 + 16 + 8 * k : tile * 16 + 24 + 8 * k, :]
                    v = jnp.where(lane >= off, v, w)
                    window = (lane >= off) | (lane < off + B - LANES)
                else:
                    window = (lane >= off) & (lane < off + B)
                v = jnp.where(window, v, 0.0)
                amount = (z0 - off + LANES) % LANES
                v = pltpu.roll(v, amount, 1)
                a = z0 // LANES
                start = z0 % LANES
                rows = pl.ds(y * 16 + 8 * k, 8)
                grid[a, rows, :] = grid[a, rows, :] + jnp.where(lane >= start, v, 0.0)
                nxt = (a + 1) % 4
                grid[nxt, rows, :] = grid[nxt, rows, :] + jnp.where(lane >= start, 0.0, v)
    for x in range(16):
        for a in range(4):
            dens[x, :, a * LANES : (a + 1) * LANES] = grid[a, pl.ds(x, 8, stride=16), :]
    rho = jnp.concatenate([grid[a] for a in range(4)], 1)
    spec = dot_left(tab_h[...], tab_l[...], rho, NT)
    slot = slot_of(lax.broadcasted_iota(jnp.int32, (LANES, LANES), 1))
    for q in range(4):
        final = spec[q * LANES : (q + 1) * LANES, :]
        for m in range(4):
            if m != q:
                part = pltpu.roll(spec[m * LANES : (m + 1) * LANES, :], (16 * (m - q)) % LANES, 1)
                final = jnp.where(slot == m, part, final)
        out[pl.ds(q, LANES, stride=4), :] = final


def patch(pieces, tab_h, tab_l):
    vm = pl.BlockSpec(memory_space=pltpu.VMEM)
    return pl.pallas_call(
        patch_kernel,
        out_shape=(
            jax.ShapeDtypeStruct((CX, CY, NZ), F32),
            jax.ShapeDtypeStruct((512, LANES), F32),
        ),
        in_specs=[vm] * 3,
        out_specs=(vm, vm),
        scratch_shapes=[pltpu.VMEM((4, LANES, LANES), F32)],
        name="patch",
    )(pieces, tab_h, tab_l)


def middle_kernel(data, kxz, ky, ry, ryt, bx, bxt, out):
    slab = jnp.concatenate([data[r * LANES : (r + 1) * LANES, :] for r in range(4)], 1)
    both = dot_left(ry[0], ry[1], slab)
    wide = lax.broadcasted_iota(jnp.int32, (1, 512), 1)
    upper = wide % LANES >= 64
    mixed = jnp.where(upper, both[256:], both[:256])
    spec = dot_right(mixed, bx[0], bx[1])
    k_square = (kxz[0:1, :] + ky[...]) + kxz[1:2, :]
    factor = jnp.where(k_square > 0, SCREEN / (k_square + SCREEN), 0.0)
    back = dot_right(spec * factor, bxt[0], bxt[1])
    both = dot_left(ryt[0], ryt[1], back)
    mixed = jnp.where(upper, both[LANES:], both[:LANES])
    for r in range(4):
        out[r * LANES : (r + 1) * LANES, :] = mixed[:, r * LANES : (r + 1) * LANES]


def middle(data, kxz, ky, ry, ryt, bx, bxt):
    vm = pl.BlockSpec(memory_space=pltpu.VMEM)
    return pl.pallas_call(
        middle_kernel,
        out_shape=jax.ShapeDtypeStruct((512, LANES), F32),
        in_specs=[vm] * 7,
        out_specs=vm,
        name="middle",
    )(data, kxz, ky, ry, ryt, bx, bxt)


def final_kernel(data, tab_h, tab_l, hart, grid):
    slot = slot_of(lax.broadcasted_iota(jnp.int32, (LANES, LANES), 1))
    parts = [data[pl.ds(q, LANES, stride=4), :] for q in range(4)]
    blocks = []
    for m in range(4):
        block = parts[m]
        for q in range(4):
            if q != m:
                block = jnp.where(slot == q, pltpu.roll(parts[q], (16 * (q - m)) % LANES, 1), block)
        blocks.append(block.T)
    spec = jnp.concatenate(blocks, 1)
    field = dot_right(spec, tab_h[...], tab_l[...])
    for a in range(4):
        grid[a] = field[:, a * LANES : (a + 1) * LANES]
    for x in range(16):
        for a in range(4):
            hart[x, :, a * LANES : (a + 1) * LANES] = grid[a, pl.ds(x, 8, stride=16), :]


def final(data, tab_h, tab_l):
    vm = pl.BlockSpec(memory_space=pltpu.VMEM)
    return pl.pallas_call(
        final_kernel,
        out_shape=jax.ShapeDtypeStruct((CX, CY, NZ), F32),
        in_specs=[vm] * 3,
        out_specs=vm,
        scratch_shapes=[pltpu.VMEM((4, LANES, LANES), F32)],
        name="final",
    )(data, tab_h, tab_l)


def real_basis(n):
    index = np.arange(n)
    angle = 2 * np.pi * (np.outer(index, index) % n) / n
    basis = np.where((index <= n // 2)[:, None], np.cos(angle), np.sin(angle)) * np.sqrt(2 / n)
    basis[0] = np.sqrt(1 / n)
    basis[n // 2] = np.where(index % 2 == 0, 1, -1) * np.sqrt(1 / n)
    return basis


def halves(table):
    table = np.ascontiguousarray(table).astype(np.float32)
    high = table.astype(BF16)
    low = (table - high.astype(np.float32)).astype(BF16)
    return high, low


def wave_square(length, positions):
    signed = np.where(positions <= length // 2, positions, positions - length)
    wave = signed.astype(np.float32) * np.float32(2 * math.pi / length)
    return wave * wave


def constants():
    rz = real_basis(NZ)
    ry = real_basis(NY).reshape(NY, 32, 2, 4).transpose(2, 0, 1, 3).reshape(2 * NY, LANES)
    ryt = ry.reshape(2, NY, LANES).transpose(0, 2, 1).reshape(2 * LANES, NY)
    rx = real_basis(NX).reshape(NX, 4, 16)
    bx = np.einsum("krx,mn->rmxnk", rx, np.eye(4))
    bx = np.broadcast_to(bx[:, None], (4, 2, 4, 16, 4, NX)).reshape(512, 256)
    return dict(
        rz=halves(rz),
        ry=np.stack(halves(ry)),
        ryt=np.stack(halves(ryt)),
        bx=np.stack(halves(bx)),
        bxt=np.stack(halves(bx.T)),
        eye=np.eye(LANES).astype(BF16),
        sel=(np.arange(LANES)[None, :] % 8 == np.arange(8)[:, None]).astype(BF16),
        ky=wave_square(NY, np.arange(NY)).reshape(NY, 1),
        kx=np.tile(wave_square(NX, np.arange(NX)), 4),
        kz=wave_square(NZ, np.arange(NZ)),
    )


def passed_along(value, axis, by):
    peers = lax.axis_size(axis)
    return lax.ppermute(value, axis, [(i, (i + by) % peers) for i in range(peers)])


def shards(orbitals, potential_boxes, corners, signs, counts):
    tab = constants()
    meta = jnp.stack(
        [
            corners[0, 0] % CX,
            corners[0, 1] % CY,
            corners[0, 2],
            counts[0],
            counts[1],
            signs[0],
            signs[1],
            lax.axis_index("row").astype(jnp.int32),
        ]
    )
    filtered, send = filter_and_box(
        meta, orbitals.reshape(16, B, YZ), potential_boxes, tab["eye"], tab["sel"]
    )
    parts = [send[0]] + [passed_along(send[j], "col", j) for j in range(1, 7)]
    pieces = lax.all_to_all(
        jnp.stack(parts, axis=1), "row", split_axis=0, concat_axis=0, tiled=True
    ).reshape(28, PIECE, LANES)
    density, packed = patch(pieces, *tab["rz"])
    packed = lax.all_to_all(packed, BOTH, split_axis=0, concat_axis=0, tiled=True)
    device = lax.axis_index("row") * 32 + lax.axis_index("col")
    kz = lax.dynamic_slice(jnp.asarray(tab["kz"]).reshape(4, LANES), (0, device), (4, 1))
    kxz = jnp.stack([jnp.asarray(tab["kx"]), jnp.repeat(kz[:, 0], NX)])
    packed = middle(packed, kxz, tab["ky"], tab["ry"], tab["ryt"], tab["bx"], tab["bxt"])
    packed = lax.all_to_all(packed, BOTH, split_axis=0, concat_axis=0, tiled=True)
    hartree = final(packed, *tab["rz"])
    return (filtered.reshape(2, ORB, B, YZ), density, hartree)


def solution(mesh):
    return jax.shard_map(
        shards,
        mesh=mesh,
        in_specs=(
            P(BOTH, None, None, None),
            P(BOTH, None, None),
            P(BOTH, None),
            P(BOTH),
            P(BOTH),
        ),
        out_specs=(
            P(BOTH, None, None, None),
            P("row", "col", None),
            P("row", "col", None),
        ),
        check_vma=False,
    )
```

```python
import math

import jax
import jax.numpy as jnp
import numpy as np
from jax import lax
from jax.experimental import pallas as pl
from jax.experimental.pallas import tpu as pltpu
from jax.sharding import PartitionSpec as P

B = 48
YZ = B * B
TILES = YZ // 128
ORB = 8
LANES = 128
NX, NY, NZ = 64, 256, 512
CX, CY = 16, 8
SCREEN = 0.0025
BOTH = ("row", "col")
F32 = jnp.float32
BF16 = jnp.bfloat16

ROOTS = [7.5 * math.cos(math.pi * k / 12) for k in (1, 11, 5, 9, 3, 7)]
KAPPA = 32.0 / 7.5**6
UNROLL = 4
PIECE = 64
BITS = 14
NT = (((1,), (1,)), ((), ()))
NN = (((1,), (0,)), ((), ()))


def dot(a, b, dims=NN):
    return lax.dot_general(a, b, dims, preferred_element_type=F32)


def split(v):
    high = v.astype(BF16)
    return high, (v - high.astype(F32)).astype(BF16)


def dot_left(tab_h, tab_l, v, dims=NN):
    h, l = split(v)
    return dot(tab_h, h, dims) + (dot(tab_h, l, dims) + dot(tab_l, h, dims))


def dot_right(v, tab_h, tab_l, dims=NN):
    h, l = split(v)
    return dot(h, tab_h, dims) + (dot(l, tab_h, dims) + dot(h, tab_l, dims))


def cheb_kernel(
    corners, signs, counts, orb_hbm, pot_hbm, eye, sel, *refs
):
    filt_hbm, sends, scratch = refs[0], refs[1:5], refs[5:]
    orb, pot, filt, buf_a, buf_b, diag, stages, box, sems = scratch
    lane = lax.broadcasted_iota(jnp.int32, (8, LANES), 1)
    sub = lax.broadcasted_iota(jnp.int32, (8, LANES), 0)
    first_x = lane % 8 == 0
    last_x = lane % 8 == 7
    zero = jnp.zeros((8, LANES), F32)
    pot_copy = pltpu.make_async_copy(pot_hbm, pot, sems.at[0])
    orb_copy = pltpu.make_async_copy(orb_hbm, orb, sems.at[1])
    pot_copy.start()
    orb_copy.start()
    for buf in (buf_a, buf_b):
        for xi in range(6):
            for k in range(6):
                buf[xi, 8 * k : 8 * k + 8, :] = zero
                buf[xi, 48 + YZ + 8 * k : 56 + YZ + 8 * k, :] = zero

    @pl.loop(0, 26)
    def _(t):
        for k in range(10):
            box[t, 8 * k : 8 * k + 8, :] = zero

    pot_copy.wait()

    @pl.loop(0, TILES // 2)
    def _(pair):
        for h in range(2):
            start = pl.multiple_of((2 * pair + h) * LANES, LANES)
            stage = stages.at[h]
            for f in range(2):
                stage[f * B : (f + 1) * B, :] = 4.5 - 2.0 * pot[f, :, pl.ds(start, LANES)]
            for xi in range(6):
                part = [stage[pl.ds(f * B + xi, 8, stride=6), :] for f in range(2)]
                block = jnp.concatenate([part[0]] * 8 + [part[1]] * 8, 0)
                diag[xi, pl.ds(start, LANES), :] = block.T

    orb_copy.wait()

    @pl.loop(0, TILES // 2)
    def _(pair):
        for h in range(2):
            start = pl.multiple_of((2 * pair + h) * LANES, LANES)
            stage = stages.at[h]
            for fo in range(16):
                stage[fo * B : (fo + 1) * B, :] = orb[fo, :, pl.ds(start, LANES)].astype(F32)
            for xi in range(6):
                block = jnp.concatenate(
                    [stage[pl.ds(fo * B + xi, 8, stride=6), :] for fo in range(16)], 0
                )
                out = dot(eye[...], block.astype(BF16), NT)
                buf_a[xi, pl.ds(pl.multiple_of(48 + start, 16), LANES), :] = out

    def apply(src, dst, root, acc):
        def rows(group, acc):
            base = pl.multiple_of(48 + 48 * UNROLL * group, 16)
            dbase = pl.multiple_of(48 * UNROLL * group, 16)
            for zt in range(6):
                mids = [
                    [src[xi, pl.ds(base + 48 * (u - 1) + 8 * zt, 8), :] for xi in range(6)]
                    for u in range(UNROLL + 2)
                ]
                for u in range(UNROLL):
                    r = base + 48 * u + 8 * zt
                    mid = mids[u + 1]
                    low = jnp.where(first_x, 0.0, pltpu.roll(mid[5], 1, 1))
                    high = jnp.where(last_x, 0.0, pltpu.roll(mid[0], LANES - 1, 1))
                    for xi in range(6):
                        below = src[xi, pl.ds(r - 1, 8), :]
                        above = src[xi, pl.ds(r + 1, 8), :]
                        if zt == 0:
                            below = jnp.where(sub == 0, 0.0, below)
                        if zt == 5:
                            above = jnp.where(sub == 7, 0.0, above)
                        beside = (mids[u][xi] + mids[u + 2][xi]) + (below + above)
                        left = mid[xi - 1] if xi > 0 else low
                        right = mid[xi + 1] if xi < 5 else high
                        beside = beside + (left + right)
                        d = diag[xi, pl.ds(dbase + 48 * u + 8 * zt, 8), :]
                        out = (d - root) * mid[xi] + beside
                        dst[xi, pl.ds(r, 8), :] = out
                        if acc is not None:
                            acc = acc + out * out
            return acc

        if acc is None:

            @pl.loop(0, B // UNROLL)
            def _(group):
                rows(group, None)

            return None
        return lax.fori_loop(0, B // UNROLL, rows, acc)

    apply(buf_a, buf_b, ROOTS[0], None)
    apply(buf_b, buf_a, ROOTS[1], None)
    apply(buf_a, buf_b, ROOTS[2], None)
    apply(buf_b, buf_a, ROOTS[3], None)
    apply(buf_a, buf_b, ROOTS[4], None)
    total = apply(buf_b, buf_a, ROOTS[5], zero)

    total = jnp.broadcast_to(jnp.sum(total, axis=0, keepdims=True), (8, LANES))
    for step in (1, 2, 4):
        other = jnp.where(
            lane & step == 0,
            pltpu.roll(total, LANES - step, 1),
            pltpu.roll(total, step, 1),
        )
        total = total + other
    scale = KAPPA * lax.rsqrt(total * (KAPPA * KAPPA / B**3) + 1e-6)
    second = lane >= 64
    count = jnp.where(second, counts[1], counts[0])
    sign = jnp.where(second, signs[1], signs[0]).astype(F32)
    scale = jnp.where((lane // 8) % 8 < count, scale, 0.0)
    weight = (scale * scale * sign)[:1, :]
    scale = scale[:1, :]

    @pl.loop(0, TILES // 2)
    def _(pair):
        for h in range(2):
            t = 2 * pair + h
            start = pl.multiple_of(t * LANES, LANES)
            for xi in range(6):
                field = buf_a[xi, pl.ds(pl.multiple_of(48 + start, 16), LANES), :]
                filt[xi, pl.ds(start, LANES), :] = (field * scale).astype(BF16)
                dh, dl = split(field * field * weight)
                dens = dot(sel[...], jnp.concatenate([dh, dl], 1), NT)
                box[t + 4, pl.ds(16 + xi, 8, stride=6), :] = dens

    filt_copy = pltpu.make_async_copy(filt, filt_hbm, sems.at[0])
    filt_copy.start()
    shift_x = lax.rem(corners[0, 0], CX)
    lanes_y = lax.rem(corners[0, 1], CY) * B
    whole = lanes_y // LANES
    rest = lax.rem(lanes_y, LANES)
    keep = lane < LANES - rest
    tall = lax.broadcasted_iota(jnp.int32, (16, LANES), 0)
    for j in range(7):
        info = jnp.full((16, LANES), corners[0, 2], jnp.int32)
        for tt in range(3):
            t0 = 3 * j + tt - whole + 4
            vals = []
            for k in range(8):
                rows = pl.ds(16 + 8 * k - shift_x, 8)
                merged = jnp.where(keep, box[t0, rows, :], box[t0 - 1, rows, :])
                vals.append(pltpu.roll(merged, rest, 1))
            top = [jnp.abs(v) for v in vals]
            while len(top) > 1:
                top = [jnp.maximum(top[n], top[n + 1]) for n in range(0, len(top), 2)]
            top = jnp.maximum(jnp.max(top[0], axis=0, keepdims=True), 1e-30)
            power = jnp.ceil(jnp.log2(jnp.broadcast_to(top, (8, LANES))))
            factor = jnp.exp2(BITS - power)
            exponent = jnp.broadcast_to(power[:1, :], (16, LANES)).astype(jnp.int32)
            info = jnp.where(tall == tt, exponent, info)
            for i in range(4):
                code = []
                for v in vals[2 * i : 2 * i + 2]:
                    v = v * factor
                    code.append((v + jnp.where(v < 0, -0.5, 0.5)).astype(jnp.int32))
                code = jnp.concatenate(code, 0).astype(jnp.int16)
                sends[i][j, 16 * tt : 16 * tt + 16, :] = code
        for i in range(4):
            sends[i][j, 48:64, :] = info.astype(jnp.int16)
    filt_copy.wait()


def filter_and_box(corners, signs, counts, orbitals, potential, eye, sel):
    vm = pl.BlockSpec(memory_space=pltpu.VMEM)
    sm = pl.BlockSpec(memory_space=pltpu.SMEM)
    hbm = pl.BlockSpec(memory_space=pl.ANY)
    return pl.pallas_call(
        cheb_kernel,
        out_shape=[jax.ShapeDtypeStruct((6, YZ, LANES), BF16)]
        + [jax.ShapeDtypeStruct((7, PIECE, LANES), jnp.int16)] * 4,
        in_specs=[sm, sm, sm, hbm, hbm, vm, vm],
        out_specs=[hbm] + [vm] * 4,
        scratch_shapes=[
            pltpu.VMEM((16, B, YZ), BF16),
            pltpu.VMEM((2, B, YZ), F32),
            pltpu.VMEM((6, YZ, LANES), BF16),
            pltpu.VMEM((6, YZ + 96, LANES), F32),
            pltpu.VMEM((6, YZ + 96, LANES), F32),
            pltpu.VMEM((6, YZ, LANES), F32),
            pltpu.VMEM((2, 16 * B, LANES), F32),
            pltpu.VMEM((26, 80, LANES), F32),
            pltpu.SemaphoreType.DMA((2,)),
        ],
        compiler_params=pltpu.CompilerParams(vmem_limit_bytes=60 * 1024 * 1024),
        name="cheb",
    )(corners, signs, counts, orbitals, potential, eye, sel)


def natural_kernel(field, eye, out, stages):
    for h in range(3):
        stage = stages.at[h]
        cells = slice(h * LANES, (h + 1) * LANES)
        for xi in range(6):
            turned = dot(eye[...], field[xi, cells, :], NT)
            for fo in range(16):
                stage[pl.ds(fo * B + xi, 8, stride=6), :] = turned[8 * fo : 8 * fo + 8, :]
        for fo in range(16):
            out[fo, :, cells] = stage[fo * B : (fo + 1) * B, :].astype(BF16)


def natural(field, eye):
    return pl.pallas_call(
        natural_kernel,
        grid=(TILES // 3,),
        out_shape=jax.ShapeDtypeStruct((16, B, YZ), BF16),
        in_specs=[
            pl.BlockSpec((6, 3 * LANES, LANES), lambda t: (0, t, 0)),
            pl.BlockSpec((LANES, LANES), lambda t: (0, 0)),
        ],
        out_specs=pl.BlockSpec((16, B, 3 * LANES), lambda t: (0, 0, t)),
        scratch_shapes=[pltpu.VMEM((3, 16 * B, LANES), F32)],
        cost_estimate=pl.CostEstimate(
            flops=2 * 108 * 128**3, bytes_accessed=4 * 16 * B * YZ, transcendentals=0
        ),
        name="natural",
    )(field, eye)


def slot_of(lane):
    return (lane // 16) % 4


def patch_kernel(*refs):
    tab_h, tab_l, dens, out, grid = refs[10:]
    lane = lax.broadcasted_iota(jnp.int32, (8, LANES), 1)
    zero = jnp.zeros((8, LANES), F32)
    for a in range(4):
        for k in range(16):
            grid[a, 8 * k : 8 * k + 8, :] = zero
    pieces = [(u, 0) for u in refs[:4]]
    pieces += [(q, n) for q in refs[4:10] for n in range(4)]
    infos = [ref[n, 48:64, :].astype(jnp.int32) for ref, n in pieces]
    zs = [jnp.max(info[3:4, :]) for info in infos]
    for (ref, n), info, z0 in zip(pieces, infos, zs):
        tiles = []
        for tt in range(3):
            factor = jnp.exp2(info[tt : tt + 1, :].astype(F32) - BITS)
            tiles.append(ref[n, 16 * tt : 16 * tt + 16, :].astype(jnp.int32).astype(F32) * factor)
        a = z0 // LANES
        nxt = lax.rem(a + 1, 4)
        start = lax.rem(z0, LANES)
        stays = lane >= start
        for k in range(2):
            moved = []
            for y in range(8):
                tile, off = (B * y) // LANES, (B * y) % LANES
                v = tiles[tile][8 * k : 8 * k + 8, :]
                if off + B > LANES:
                    v = jnp.where(lane >= off, v, tiles[tile + 1][8 * k : 8 * k + 8, :])
                    window = (lane >= off) | (lane < off + B - LANES)
                else:
                    window = (lane >= off) & (lane < off + B)
                v = jnp.where(window, v, 0.0)
                moved.append(pltpu.roll(v, lax.rem(z0 + (LANES - off), LANES), 1))
            here = [grid[a, y * 16 + 8 * k : y * 16 + 8 * k + 8, :] for y in range(8)]
            there = [grid[nxt, y * 16 + 8 * k : y * 16 + 8 * k + 8, :] for y in range(8)]
            for y in range(8):
                rows = slice(y * 16 + 8 * k, y * 16 + 8 * k + 8)
                grid[a, rows, :] = here[y] + jnp.where(stays, moved[y], 0.0)
                grid[nxt, rows, :] = there[y] + jnp.where(stays, 0.0, moved[y])
    for x in range(16):
        for a in range(4):
            dens[x, :, a * LANES : (a + 1) * LANES] = grid[a, pl.ds(x, 8, stride=16), :]
    rho = jnp.concatenate([grid[a] for a in range(4)], 1)
    rho_h, rho_l = split(rho)
    wide = dot(tab_h[...], jnp.concatenate([rho_h, rho_l], 0), NT)
    spec = wide[:, :LANES] + (wide[:, LANES:] + dot(tab_l[...], rho_h, NT))
    slot = slot_of(lax.broadcasted_iota(jnp.int32, (LANES, LANES), 1))
    for q in range(4):
        final = spec[q * LANES : (q + 1) * LANES, :]
        for m in range(4):
            if m != q:
                part = pltpu.roll(spec[m * LANES : (m + 1) * LANES, :], (16 * (m - q)) % LANES, 1)
                final = jnp.where(slot == m, part, final)
        out[pl.ds(q, LANES, stride=4), :] = final


def patch(pieces, tab_h, tab_l):
    def first(count):
        return pl.BlockSpec((count, PIECE, LANES), lambda i: (0, 0, 0))

    def whole(*shape):
        return pl.BlockSpec(shape, lambda i: (0,) * len(shape))

    return pl.pallas_call(
        patch_kernel,
        grid=(1,),
        out_shape=(
            jax.ShapeDtypeStruct((CX, CY, NZ), F32),
            jax.ShapeDtypeStruct((512, LANES), F32),
        ),
        in_specs=[first(1)] * 4 + [first(4)] * 6 + [whole(512, 512)] * 2,
        out_specs=(whole(CX, CY, NZ), whole(512, LANES)),
        scratch_shapes=[pltpu.VMEM((4, LANES, LANES), F32)],
        name="patch",
    )(*pieces, tab_h, tab_l)


def wave(length, position):
    signed = jnp.where(position <= length // 2, position, position - length)
    k = signed.astype(F32) * (2 * math.pi / length)
    return k * k


def middle_kernel(data, ry, ryt, bx, bxt, out):
    slab = jnp.concatenate([data[r * LANES : (r + 1) * LANES, :] for r in range(4)], 1)
    both = dot_left(ry[0], ry[1], slab)
    wide = lax.broadcasted_iota(jnp.int32, (1, 512), 1)
    upper = wide % LANES >= 64
    mixed = jnp.where(upper, both[256:], both[:256])
    spec = dot_right(mixed, bx[0], bx[1])
    column = lax.broadcasted_iota(jnp.int32, (1, 256), 1)
    device = lax.axis_index("row") * 32 + lax.axis_index("col")
    kx = wave(NX, column % NX)
    kz = wave(NZ, (column // NX) * LANES + device)
    ky = wave(NY, lax.broadcasted_iota(jnp.int32, (NY, 256), 0))
    k_square = (kx + ky) + kz
    factor = jnp.where(k_square > 0, SCREEN / (k_square + SCREEN), 0.0)
    back = dot_right(spec * factor, bxt[0], bxt[1])
    both = dot_left(ryt[0], ryt[1], back)
    mixed = jnp.where(upper, both[LANES:], both[:LANES])
    for r in range(4):
        out[r * LANES : (r + 1) * LANES, :] = mixed[:, r * LANES : (r + 1) * LANES]


def middle(data, ry, ryt, bx, bxt):
    vm = pl.BlockSpec(memory_space=pltpu.VMEM)
    return pl.pallas_call(
        middle_kernel,
        out_shape=jax.ShapeDtypeStruct((512, LANES), F32),
        in_specs=[vm] * 5,
        out_specs=vm,
        name="middle",
    )(data, ry, ryt, bx, bxt)


def final_kernel(data, tab_h, tab_l, hart, grid):
    slot = slot_of(lax.broadcasted_iota(jnp.int32, (LANES, LANES), 1))
    parts = [data[pl.ds(q, LANES, stride=4), :] for q in range(4)]
    blocks = []
    for m in range(4):
        block = parts[m]
        for q in range(4):
            if q != m:
                block = jnp.where(slot == q, pltpu.roll(parts[q], (16 * (q - m)) % LANES, 1), block)
        blocks.append(block.T)
    spec = jnp.concatenate(blocks, 1)
    field = dot_right(spec, tab_h[...], tab_l[...])
    for a in range(4):
        grid[a] = field[:, a * LANES : (a + 1) * LANES]
    for x in range(16):
        for a in range(4):
            hart[x, :, a * LANES : (a + 1) * LANES] = grid[a, pl.ds(x, 8, stride=16), :]


def final(data, tab_h, tab_l):
    vm = pl.BlockSpec(memory_space=pltpu.VMEM)
    return pl.pallas_call(
        final_kernel,
        out_shape=jax.ShapeDtypeStruct((CX, CY, NZ), F32),
        in_specs=[vm] * 3,
        out_specs=vm,
        scratch_shapes=[pltpu.VMEM((4, LANES, LANES), F32)],
        name="final",
    )(data, tab_h, tab_l)


def real_basis(n):
    index = np.arange(n)
    angle = 2 * np.pi * (np.outer(index, index) % n) / n
    basis = np.where((index <= n // 2)[:, None], np.cos(angle), np.sin(angle)) * np.sqrt(2 / n)
    basis[0] = np.sqrt(1 / n)
    basis[n // 2] = np.where(index % 2 == 0, 1, -1) * np.sqrt(1 / n)
    return basis


def halves(table):
    table = np.ascontiguousarray(table).astype(np.float32)
    high = table.astype(BF16)
    low = (table - high.astype(np.float32)).astype(BF16)
    return high, low


def constants():
    rz = real_basis(NZ)
    ry = real_basis(NY).reshape(NY, 32, 2, 4).transpose(2, 0, 1, 3).reshape(2 * NY, LANES)
    ryt = ry.reshape(2, NY, LANES).transpose(0, 2, 1).reshape(2 * LANES, NY)
    rx = real_basis(NX).reshape(NX, 4, 16)
    bx = np.einsum("krx,mn->rmxnk", rx, np.eye(4))
    bx = np.broadcast_to(bx[:, None], (4, 2, 4, 16, 4, NX)).reshape(512, 256)
    return dict(
        rz=halves(rz),
        ry=np.stack(halves(ry)),
        ryt=np.stack(halves(ryt)),
        bx=np.stack(halves(bx)),
        bxt=np.stack(halves(bx.T)),
        eye=np.eye(LANES).astype(BF16),
        sel=(np.arange(2 * LANES)[None, :] % 8 == np.arange(8)[:, None]).astype(BF16),
    )


def passed_along(value, axis, by):
    peers = lax.axis_size(axis)
    return lax.ppermute(value, axis, [(i, (i + by) % peers) for i in range(peers)])


def shards(orbitals, potential_boxes, corners, signs, counts):
    tab = constants()
    field, *send = filter_and_box(
        corners,
        signs,
        counts,
        orbitals.reshape(16, B, YZ),
        potential_boxes,
        tab["eye"],
        tab["sel"],
    )
    filtered = natural(field, tab["eye"])
    rows = [send[0]] + [passed_along(send[i], "row", i) for i in range(1, 4)]
    got = [
        passed_along(jnp.concatenate([u[j : j + 1] for u in rows]), "col", j) for j in range(1, 7)
    ]
    density, packed = patch((*rows, *got), *tab["rz"])
    packed = lax.all_to_all(packed, BOTH, split_axis=0, concat_axis=0, tiled=True)
    packed = middle(packed, tab["ry"], tab["ryt"], tab["bx"], tab["bxt"])
    packed = lax.all_to_all(packed, BOTH, split_axis=0, concat_axis=0, tiled=True)
    hartree = final(packed, *tab["rz"])
    return (filtered.reshape(2, ORB, B, YZ), density, hartree)


def solution(mesh):
    return jax.shard_map(
        shards,
        mesh=mesh,
        in_specs=(
            P(BOTH, None, None, None),
            P(BOTH, None, None),
            P(BOTH, None),
            P(BOTH),
            P(BOTH),
        ),
        out_specs=(
            P(BOTH, None, None, None),
            P("row", "col", None),
            P("row", "col", None),
        ),
        check_vma=False,
    )
```

```python
import math

import jax
import jax.numpy as jnp
import numpy as np
from jax import lax
from jax.experimental import pallas as pl
from jax.experimental.pallas import tpu as pltpu
from jax.sharding import PartitionSpec as P

B = 48
YZ = B * B
TILES = YZ // 128
ORB = 8
LANES = 128
NX, NY, NZ = 64, 256, 512
CX, CY = 16, 8
SCREEN = 0.0025
BOTH = ("row", "col")
F32 = jnp.float32
BF16 = jnp.bfloat16

ROOTS = [7.5 * math.cos(math.pi * k / 12) for k in (1, 11, 5, 9, 3, 7)]
KAPPA = 32.0 / 7.5**6
UNROLL = 4
PIECE = 64
BITS = 14
NT = (((1,), (1,)), ((), ()))
NN = (((1,), (0,)), ((), ()))


def dot(a, b, dims=NN):
    return lax.dot_general(a, b, dims, preferred_element_type=F32)


def split(v):
    high = v.astype(BF16)
    return high, (v - high.astype(F32)).astype(BF16)


def dot_left(tab_h, tab_l, v, dims=NN):
    h, l = split(v)
    return dot(tab_h, h, dims) + (dot(tab_h, l, dims) + dot(tab_l, h, dims))


def dot_right(v, tab_h, tab_l, dims=NN):
    h, l = split(v)
    return dot(h, tab_h, dims) + (dot(l, tab_h, dims) + dot(h, tab_l, dims))


def cheb_kernel(
    corners, signs, counts, orb_hbm, pot_hbm, eye, sel, *refs
):
    filt_hbm, sends, scratch = refs[0], refs[1:5], refs[5:]
    orb, pot, filt, buf_a, buf_b, diag, stages, box, sems = scratch
    lane = lax.broadcasted_iota(jnp.int32, (8, LANES), 1)
    sub = lax.broadcasted_iota(jnp.int32, (8, LANES), 0)
    first_x = lane % 8 == 0
    last_x = lane % 8 == 7
    zero = jnp.zeros((8, LANES), F32)
    third = YZ // 3

    def incoming(c):
        cells = pl.ds(pl.multiple_of(c * third, third), third)
        return (
            pltpu.make_async_copy(pot_hbm.at[:, :, cells], pot.at[:, :, cells], sems.at[0, c]),
            pltpu.make_async_copy(orb_hbm.at[:, :, cells], orb.at[:, :, cells], sems.at[1, c]),
        )

    def outgoing(c):
        cells = pl.ds(pl.multiple_of(c * third, third), third)
        return pltpu.make_async_copy(filt.at[:, cells, :], filt_hbm.at[:, cells, :], sems.at[0, c])

    for c in range(3):
        for copy in incoming(c):
            copy.start()
    for buf in (buf_a, buf_b):
        for xi in range(6):
            for k in range(6):
                buf[xi, 8 * k : 8 * k + 8, :] = zero
                buf[xi, 48 + YZ + 8 * k : 56 + YZ + 8 * k, :] = zero

    @pl.loop(0, 26)
    def _(t):
        for k in range(10):
            box[t, 8 * k : 8 * k + 8, :] = zero

    @pl.loop(0, 3)
    def _(c):
        for copy in incoming(c):
            copy.wait()

        @pl.loop(3 * c, 3 * c + 3)
        def _(pair):
            for h in range(2):
                start = pl.multiple_of((2 * pair + h) * LANES, LANES)
                stage = stages.at[2 + h]
                for f in range(2):
                    stage[f * B : (f + 1) * B, :] = 4.5 - 2.0 * pot[f, :, pl.ds(start, LANES)]
                for xi in range(6):
                    part = [stage[pl.ds(f * B + xi, 8, stride=6), :] for f in range(2)]
                    block = jnp.concatenate([part[0]] * 8 + [part[1]] * 8, 0)
                    diag[xi, pl.ds(start, LANES), :] = block.T
                stage = stages.at[h]
                for fo in range(16):
                    stage[fo * B : (fo + 1) * B, :] = orb[fo, :, pl.ds(start, LANES)].astype(F32)
                for xi in range(6):
                    block = jnp.concatenate(
                        [stage[pl.ds(fo * B + xi, 8, stride=6), :] for fo in range(16)], 0
                    )
                    out = dot(eye[...], block.astype(BF16), NT)
                    buf_a[xi, pl.ds(pl.multiple_of(48 + start, 16), LANES), :] = out

    def apply(src, dst, root, acc):
        def rows(group, acc):
            base = pl.multiple_of(48 + 48 * UNROLL * group, 16)
            dbase = pl.multiple_of(48 * UNROLL * group, 16)
            for zt in range(6):
                first = base + 8 * zt

                def load(u):
                    return [src[xi, pl.ds(first + 48 * u, 8), :] for xi in range(6)]

                def past_last(mid):
                    return jnp.where(last_x, 0.0, pltpu.roll(mid[0], LANES - 1, 1))

                before, nxt = load(-1), load(0)
                ends = nxt[1:] + [past_last(nxt)]
                diag_before = [before[xi] + ends[xi] for xi in range(6)]
                for u in range(UNROLL):
                    r = first + 48 * u
                    mid, nxt = nxt, load(u + 1)
                    low = jnp.where(first_x, 0.0, pltpu.roll(mid[5], 1, 1))
                    diag_here = [low + nxt[0]] + [mid[xi] + nxt[xi + 1] for xi in range(5)]
                    for xi in range(6):
                        below = src[xi, pl.ds(r - 1, 8), :]
                        above = src[xi, pl.ds(r + 1, 8), :]
                        if zt == 0:
                            below = jnp.where(sub == 0, 0.0, below)
                        if zt == 5:
                            above = jnp.where(sub == 7, 0.0, above)
                        beside = (diag_here[xi] + diag_before[xi]) + (below + above)
                        d = diag[xi, pl.ds(dbase + 48 * u + 8 * zt, 8), :]
                        out = (d - root) * mid[xi] + beside
                        dst[xi, pl.ds(r, 8), :] = out
                        if acc is not None:
                            acc = acc + out * out
                    if u < UNROLL - 1:
                        diag_before = diag_here[1:] + [mid[5] + past_last(nxt)]
            return acc

        if acc is None:

            @pl.loop(0, B // UNROLL)
            def _(group):
                rows(group, None)

            return None
        return lax.fori_loop(0, B // UNROLL, rows, acc)

    apply(buf_a, buf_b, ROOTS[0], None)
    apply(buf_b, buf_a, ROOTS[1], None)
    apply(buf_a, buf_b, ROOTS[2], None)
    apply(buf_b, buf_a, ROOTS[3], None)
    apply(buf_a, buf_b, ROOTS[4], None)
    total = apply(buf_b, buf_a, ROOTS[5], zero)

    total = jnp.broadcast_to(jnp.sum(total, axis=0, keepdims=True), (8, LANES))
    for step in (1, 2, 4):
        other = jnp.where(
            lane & step == 0,
            pltpu.roll(total, LANES - step, 1),
            pltpu.roll(total, step, 1),
        )
        total = total + other
    scale = KAPPA * lax.rsqrt(total * (KAPPA * KAPPA / B**3) + 1e-6)
    second = lane >= 64
    count = jnp.where(second, counts[1], counts[0])
    sign = jnp.where(second, signs[1], signs[0]).astype(F32)
    scale = jnp.where((lane // 8) % 8 < count, scale, 0.0)
    weight = (scale * scale * sign)[:1, :]
    scale = scale[:1, :]

    @pl.loop(0, 3)
    def _(c):
        @pl.loop(3 * c, 3 * c + 3)
        def _(pair):
            for h in range(2):
                t = 2 * pair + h
                start = pl.multiple_of(t * LANES, LANES)
                for xi in range(6):
                    field = buf_a[xi, pl.ds(pl.multiple_of(48 + start, 16), LANES), :]
                    filt[xi, pl.ds(start, LANES), :] = (field * scale).astype(BF16)
                    dh, dl = split(field * field * weight)
                    dens = dot(sel[...], jnp.concatenate([dh, dl], 1), NT)
                    box[t + 4, pl.ds(16 + xi, 8, stride=6), :] = dens

        outgoing(c).start()

    shift_x = lax.rem(corners[0, 0], CX)
    lanes_y = lax.rem(corners[0, 1], CY) * B
    whole = lanes_y // LANES
    rest = lax.rem(lanes_y, LANES)
    keep = lane < LANES - rest
    tall = lax.broadcasted_iota(jnp.int32, (16, LANES), 0)
    for j in range(7):
        info = jnp.full((16, LANES), corners[0, 2], jnp.int32)
        for tt in range(3):
            t0 = 3 * j + tt - whole + 4
            vals = []
            for k in range(8):
                rows = pl.ds(16 + 8 * k - shift_x, 8)
                merged = jnp.where(keep, box[t0, rows, :], box[t0 - 1, rows, :])
                vals.append(pltpu.roll(merged, rest, 1))
            top = [jnp.abs(v) for v in vals]
            while len(top) > 1:
                top = [jnp.maximum(top[n], top[n + 1]) for n in range(0, len(top), 2)]
            top = jnp.maximum(jnp.max(top[0], axis=0, keepdims=True), 1e-30)
            power = jnp.ceil(jnp.log2(jnp.broadcast_to(top, (8, LANES))))
            factor = jnp.exp2(BITS - power)
            exponent = jnp.broadcast_to(power[:1, :], (16, LANES)).astype(jnp.int32)
            info = jnp.where(tall == tt, exponent, info)
            for i in range(4):
                code = []
                for v in vals[2 * i : 2 * i + 2]:
                    v = v * factor
                    code.append((v + jnp.where(v < 0, -0.5, 0.5)).astype(jnp.int32))
                code = jnp.concatenate(code, 0).astype(jnp.int16)
                sends[i][j, 16 * tt : 16 * tt + 16, :] = code
        for i in range(4):
            sends[i][j, 48:64, :] = info.astype(jnp.int16)
    for c in range(3):
        outgoing(c).wait()


def filter_and_box(corners, signs, counts, orbitals, potential, eye, sel):
    vm = pl.BlockSpec(memory_space=pltpu.VMEM)
    sm = pl.BlockSpec(memory_space=pltpu.SMEM)
    hbm = pl.BlockSpec(memory_space=pl.ANY)
    return pl.pallas_call(
        cheb_kernel,
        out_shape=[jax.ShapeDtypeStruct((6, YZ, LANES), BF16)]
        + [jax.ShapeDtypeStruct((7, PIECE, LANES), jnp.int16)] * 4,
        in_specs=[sm, sm, sm, hbm, hbm, vm, vm],
        out_specs=[hbm] + [vm] * 4,
        scratch_shapes=[
            pltpu.VMEM((16, B, YZ), BF16),
            pltpu.VMEM((2, B, YZ), F32),
            pltpu.VMEM((6, YZ, LANES), BF16),
            pltpu.VMEM((6, YZ + 96, LANES), F32),
            pltpu.VMEM((6, YZ + 96, LANES), F32),
            pltpu.VMEM((6, YZ, LANES), F32),
            pltpu.VMEM((4, 16 * B, LANES), F32),
            pltpu.VMEM((26, 80, LANES), F32),
            pltpu.SemaphoreType.DMA((2, 3)),
        ],
        compiler_params=pltpu.CompilerParams(vmem_limit_bytes=60 * 1024 * 1024),
        name="cheb",
    )(corners, signs, counts, orbitals, potential, eye, sel)


def natural_kernel(field, eye, out, stages):
    for h in range(3):
        stage = stages.at[h]
        cells = slice(h * LANES, (h + 1) * LANES)
        for xi in range(6):
            turned = dot(eye[...], field[xi, cells, :], NT)
            for fo in range(16):
                stage[pl.ds(fo * B + xi, 8, stride=6), :] = turned[8 * fo : 8 * fo + 8, :]
        for fo in range(16):
            out[fo, :, cells] = stage[fo * B : (fo + 1) * B, :].astype(BF16)


def natural(field, eye):
    return pl.pallas_call(
        natural_kernel,
        grid=(TILES // 3,),
        out_shape=jax.ShapeDtypeStruct((16, B, YZ), BF16),
        in_specs=[
            pl.BlockSpec((6, 3 * LANES, LANES), lambda t: (0, t, 0)),
            pl.BlockSpec((LANES, LANES), lambda t: (0, 0)),
        ],
        out_specs=pl.BlockSpec((16, B, 3 * LANES), lambda t: (0, 0, t)),
        scratch_shapes=[pltpu.VMEM((3, 16 * B, LANES), F32)],
        cost_estimate=pl.CostEstimate(
            flops=2 * 108 * 128**3, bytes_accessed=4 * 16 * B * YZ, transcendentals=0
        ),
        name="natural",
    )(field, eye)


def slot_of(lane):
    return (lane // 16) % 4


def patch_kernel(*refs):
    tab_h, tab_l, dens, out, grid = refs[10:]
    lane = lax.broadcasted_iota(jnp.int32, (8, LANES), 1)
    zero = jnp.zeros((8, LANES), F32)
    for a in range(4):
        for k in range(16):
            grid[a, 8 * k : 8 * k + 8, :] = zero
    pieces = [(u, 0) for u in refs[:4]]
    pieces += [(q, n) for q in refs[4:10] for n in range(4)]
    infos = [ref[n, 48:64, :].astype(jnp.int32) for ref, n in pieces]
    zs = [jnp.max(info[3:4, :]) for info in infos]
    for (ref, n), info, z0 in zip(pieces, infos, zs):
        tiles = []
        for tt in range(3):
            factor = jnp.exp2(info[tt : tt + 1, :].astype(F32) - BITS)
            tiles.append(ref[n, 16 * tt : 16 * tt + 16, :].astype(jnp.int32).astype(F32) * factor)
        a = z0 // LANES
        nxt = lax.rem(a + 1, 4)
        start = lax.rem(z0, LANES)
        stays = lane >= start
        for k in range(2):
            moved = []
            for y in range(8):
                tile, off = (B * y) // LANES, (B * y) % LANES
                v = tiles[tile][8 * k : 8 * k + 8, :]
                if off + B > LANES:
                    v = jnp.where(lane >= off, v, tiles[tile + 1][8 * k : 8 * k + 8, :])
                    window = (lane >= off) | (lane < off + B - LANES)
                else:
                    window = (lane >= off) & (lane < off + B)
                v = jnp.where(window, v, 0.0)
                moved.append(pltpu.roll(v, lax.rem(z0 + (LANES - off), LANES), 1))
            here = [grid[a, y * 16 + 8 * k : y * 16 + 8 * k + 8, :] for y in range(8)]
            there = [grid[nxt, y * 16 + 8 * k : y * 16 + 8 * k + 8, :] for y in range(8)]
            for y in range(8):
                rows = slice(y * 16 + 8 * k, y * 16 + 8 * k + 8)
                grid[a, rows, :] = here[y] + jnp.where(stays, moved[y], 0.0)
                grid[nxt, rows, :] = there[y] + jnp.where(stays, 0.0, moved[y])
    for x in range(16):
        for a in range(4):
            dens[x, :, a * LANES : (a + 1) * LANES] = grid[a, pl.ds(x, 8, stride=16), :]
    rho = jnp.concatenate([grid[a] for a in range(4)], 1)
    rho_h, rho_l = split(rho)
    wide = dot(tab_h[...], jnp.concatenate([rho_h, rho_l], 0), NT)
    spec = wide[:, :LANES] + (wide[:, LANES:] + dot(tab_l[...], rho_h, NT))
    slot = slot_of(lax.broadcasted_iota(jnp.int32, (LANES, LANES), 1))
    for q in range(4):
        final = spec[q * LANES : (q + 1) * LANES, :]
        for m in range(4):
            if m != q:
                part = pltpu.roll(spec[m * LANES : (m + 1) * LANES, :], (16 * (m - q)) % LANES, 1)
                final = jnp.where(slot == m, part, final)
        out[pl.ds(q, LANES, stride=4), :] = final


def patch(pieces, tab_h, tab_l):
    def first(count):
        return pl.BlockSpec((count, PIECE, LANES), lambda i: (0, 0, 0))

    def whole(*shape):
        return pl.BlockSpec(shape, lambda i: (0,) * len(shape))

    return pl.pallas_call(
        patch_kernel,
        grid=(1,),
        out_shape=(
            jax.ShapeDtypeStruct((CX, CY, NZ), F32),
            jax.ShapeDtypeStruct((512, LANES), F32),
        ),
        in_specs=[first(1)] * 4 + [first(4)] * 6 + [whole(512, 512)] * 2,
        out_specs=(whole(CX, CY, NZ), whole(512, LANES)),
        scratch_shapes=[pltpu.VMEM((4, LANES, LANES), F32)],
        name="patch",
    )(*pieces, tab_h, tab_l)


def wave(length, position):
    signed = jnp.where(position <= length // 2, position, position - length)
    k = signed.astype(F32) * (2 * math.pi / length)
    return k * k


def middle_kernel(data, ry, ryt, bx, bxt, out):
    slab = jnp.concatenate([data[r * LANES : (r + 1) * LANES, :] for r in range(4)], 1)
    both = dot_left(ry[0], ry[1], slab)
    wide = lax.broadcasted_iota(jnp.int32, (1, 512), 1)
    upper = wide % LANES >= 64
    mixed = jnp.where(upper, both[256:], both[:256])
    spec = dot_right(mixed, bx[0], bx[1])
    column = lax.broadcasted_iota(jnp.int32, (1, 256), 1)
    device = lax.axis_index("row") * 32 + lax.axis_index("col")
    kx = wave(NX, column % NX)
    kz = wave(NZ, (column // NX) * LANES + device)
    ky = wave(NY, lax.broadcasted_iota(jnp.int32, (NY, 256), 0))
    k_square = (kx + ky) + kz
    factor = jnp.where(k_square > 0, SCREEN / (k_square + SCREEN), 0.0)
    back = dot_right(spec * factor, bxt[0], bxt[1])
    both = dot_left(ryt[0], ryt[1], back)
    mixed = jnp.where(upper, both[LANES:], both[:LANES])
    for r in range(4):
        out[r * LANES : (r + 1) * LANES, :] = mixed[:, r * LANES : (r + 1) * LANES]


def middle(data, ry, ryt, bx, bxt):
    vm = pl.BlockSpec(memory_space=pltpu.VMEM)
    return pl.pallas_call(
        middle_kernel,
        out_shape=jax.ShapeDtypeStruct((512, LANES), F32),
        in_specs=[vm] * 5,
        out_specs=vm,
        name="middle",
    )(data, ry, ryt, bx, bxt)


def final_kernel(data, tab_h, tab_l, hart, grid):
    slot = slot_of(lax.broadcasted_iota(jnp.int32, (LANES, LANES), 1))
    parts = [data[pl.ds(q, LANES, stride=4), :] for q in range(4)]
    blocks = []
    for m in range(4):
        block = parts[m]
        for q in range(4):
            if q != m:
                block = jnp.where(slot == q, pltpu.roll(parts[q], (16 * (q - m)) % LANES, 1), block)
        blocks.append(block.T)
    spec = jnp.concatenate(blocks, 1)
    field = dot_right(spec, tab_h[...], tab_l[...])
    for a in range(4):
        grid[a] = field[:, a * LANES : (a + 1) * LANES]
    for x in range(16):
        for a in range(4):
            hart[x, :, a * LANES : (a + 1) * LANES] = grid[a, pl.ds(x, 8, stride=16), :]


def final(data, tab_h, tab_l):
    vm = pl.BlockSpec(memory_space=pltpu.VMEM)
    return pl.pallas_call(
        final_kernel,
        out_shape=jax.ShapeDtypeStruct((CX, CY, NZ), F32),
        in_specs=[vm] * 3,
        out_specs=vm,
        scratch_shapes=[pltpu.VMEM((4, LANES, LANES), F32)],
        name="final",
    )(data, tab_h, tab_l)


def real_basis(n):
    index = np.arange(n)
    angle = 2 * np.pi * (np.outer(index, index) % n) / n
    basis = np.where((index <= n // 2)[:, None], np.cos(angle), np.sin(angle)) * np.sqrt(2 / n)
    basis[0] = np.sqrt(1 / n)
    basis[n // 2] = np.where(index % 2 == 0, 1, -1) * np.sqrt(1 / n)
    return basis


def halves(table):
    table = np.ascontiguousarray(table).astype(np.float32)
    high = table.astype(BF16)
    low = (table - high.astype(np.float32)).astype(BF16)
    return high, low


def constants():
    rz = real_basis(NZ)
    ry = real_basis(NY).reshape(NY, 32, 2, 4).transpose(2, 0, 1, 3).reshape(2 * NY, LANES)
    ryt = ry.reshape(2, NY, LANES).transpose(0, 2, 1).reshape(2 * LANES, NY)
    rx = real_basis(NX).reshape(NX, 4, 16)
    bx = np.einsum("krx,mn->rmxnk", rx, np.eye(4))
    bx = np.broadcast_to(bx[:, None], (4, 2, 4, 16, 4, NX)).reshape(512, 256)
    return dict(
        rz=halves(rz),
        ry=np.stack(halves(ry)),
        ryt=np.stack(halves(ryt)),
        bx=np.stack(halves(bx)),
        bxt=np.stack(halves(bx.T)),
        eye=np.eye(LANES).astype(BF16),
        sel=(np.arange(2 * LANES)[None, :] % 8 == np.arange(8)[:, None]).astype(BF16),
    )


def passed_along(value, axis, by):
    peers = lax.axis_size(axis)
    return lax.ppermute(value, axis, [(i, (i + by) % peers) for i in range(peers)])


def shards(orbitals, potential_boxes, corners, signs, counts):
    tab = constants()
    field, *send = filter_and_box(
        corners,
        signs,
        counts,
        orbitals.reshape(16, B, YZ),
        potential_boxes,
        tab["eye"],
        tab["sel"],
    )
    filtered = natural(field, tab["eye"])
    rows = [send[0]] + [passed_along(send[i], "row", i) for i in range(1, 4)]
    got = [
        passed_along(jnp.concatenate([u[j : j + 1] for u in rows]), "col", j) for j in range(1, 7)
    ]
    density, packed = patch((*rows, *got), *tab["rz"])
    packed = lax.all_to_all(packed, BOTH, split_axis=0, concat_axis=0, tiled=True)
    packed = middle(packed, tab["ry"], tab["ryt"], tab["bx"], tab["bxt"])
    packed = lax.all_to_all(packed, BOTH, split_axis=0, concat_axis=0, tiled=True)
    hartree = final(packed, *tab["rz"])
    return (filtered.reshape(2, ORB, B, YZ), density, hartree)


def solution(mesh):
    return jax.shard_map(
        shards,
        mesh=mesh,
        in_specs=(
            P(BOTH, None, None, None),
            P(BOTH, None, None),
            P(BOTH, None),
            P(BOTH),
            P(BOTH),
        ),
        out_specs=(
            P(BOTH, None, None, None),
            P("row", "col", None),
            P("row", "col", None),
        ),
        check_vma=False,
    )
```

```python
import math

import jax
import jax.numpy as jnp
import numpy as np
from jax import lax
from jax.experimental import pallas as pl
from jax.experimental.pallas import tpu as pltpu
from jax.sharding import PartitionSpec as P

B = 48
YZ = B * B
TILES = YZ // 128
ORB = 8
LANES = 128
NX, NY, NZ = 64, 256, 512
CX, CY = 16, 8
SCREEN = 0.0025
BOTH = ("row", "col")
F32 = jnp.float32
BF16 = jnp.bfloat16

ROOTS = [7.5 * math.cos(math.pi * k / 12) for k in (1, 11, 5, 9, 3, 7)]
KAPPA = 32.0 / 7.5**6
UNROLL = 4
PIECE = 64
BITS = 14
NT = (((1,), (1,)), ((), ()))
NN = (((1,), (0,)), ((), ()))


def dot(a, b, dims=NN):
    return lax.dot_general(a, b, dims, preferred_element_type=F32)


def split(v):
    high = v.astype(BF16)
    return high, (v - high.astype(F32)).astype(BF16)


def dot_left(tab_h, tab_l, v, dims=NN):
    h, l = split(v)
    return dot(tab_h, h, dims) + (dot(tab_h, l, dims) + dot(tab_l, h, dims))


def dot_right(v, tab_h, tab_l, dims=NN):
    h, l = split(v)
    return dot(h, tab_h, dims) + (dot(l, tab_h, dims) + dot(h, tab_l, dims))


def cheb_kernel(
    corners, signs, counts, orb_hbm, pot_hbm, eye, sel, *refs
):
    filt_hbm, sends, scratch = refs[0], refs[1:5], refs[5:]
    orb, pot, filt, buf_a, buf_b, diag, stages, box, sems = scratch
    lane = lax.broadcasted_iota(jnp.int32, (8, LANES), 1)
    sub = lax.broadcasted_iota(jnp.int32, (8, LANES), 0)
    first_x = lane % 8 == 0
    last_x = lane % 8 == 7
    zero = jnp.zeros((8, LANES), F32)
    third = YZ // 3

    def incoming(c):
        cells = pl.ds(pl.multiple_of(c * third, third), third)
        return (
            pltpu.make_async_copy(pot_hbm.at[:, :, cells], pot.at[:, :, cells], sems.at[0, c]),
            pltpu.make_async_copy(orb_hbm.at[:, :, cells], orb.at[:, :, cells], sems.at[1, c]),
        )

    def outgoing(c):
        cells = pl.ds(pl.multiple_of(c * third, third), third)
        return pltpu.make_async_copy(filt.at[:, cells, :], filt_hbm.at[:, cells, :], sems.at[0, c])

    for c in range(3):
        for copy in incoming(c):
            copy.start()
    for buf in (buf_a, buf_b):
        for xi in range(6):
            for k in range(6):
                buf[xi, 8 * k : 8 * k + 8, :] = zero
                buf[xi, 48 + YZ + 8 * k : 56 + YZ + 8 * k, :] = zero

    @pl.loop(0, 26)
    def _(t):
        for k in range(10):
            box[t, 8 * k : 8 * k + 8, :] = zero

    @pl.loop(0, 3)
    def _(c):
        for copy in incoming(c):
            copy.wait()

        @pl.loop(3 * c, 3 * c + 3)
        def _(pair):
            for h in range(2):
                start = pl.multiple_of((2 * pair + h) * LANES, LANES)
                stage = stages.at[2 + h]
                for f in range(2):
                    stage[f * B : (f + 1) * B, :] = 4.5 - 2.0 * pot[f, :, pl.ds(start, LANES)]
                for xi in range(6):
                    part = [stage[pl.ds(f * B + xi, 8, stride=6), :] for f in range(2)]
                    block = jnp.concatenate([part[0]] * 8 + [part[1]] * 8, 0)
                    diag[xi, pl.ds(start, LANES), :] = block.T
                stage = stages.at[h]
                for fo in range(16):
                    stage[fo * B : (fo + 1) * B, :] = orb[fo, :, pl.ds(start, LANES)].astype(F32)
                for xi in range(6):
                    block = jnp.concatenate(
                        [stage[pl.ds(fo * B + xi, 8, stride=6), :] for fo in range(16)], 0
                    )
                    out = dot(eye[...], block.astype(BF16), NT)
                    buf_a[xi, pl.ds(pl.multiple_of(48 + start, 16), LANES), :] = out

    def apply(src, dst, root, acc):
        def rows(group, acc):
            acc = None if acc is None else list(acc)
            base = pl.multiple_of(48 + 48 * UNROLL * group, 16)
            dbase = pl.multiple_of(48 * UNROLL * group, 16)
            for zt in range(6):
                first = base + 8 * zt

                def load(u):
                    return [src[xi, pl.ds(first + 48 * u, 8), :] for xi in range(6)]

                def past_last(mid):
                    return jnp.where(last_x, 0.0, pltpu.roll(mid[0], LANES - 1, 1))

                before, nxt = load(-1), load(0)
                ends = nxt[1:] + [past_last(nxt)]
                diag_before = [before[xi] + ends[xi] for xi in range(6)]
                for u in range(UNROLL):
                    r = first + 48 * u
                    mid, nxt = nxt, load(u + 1)
                    low = jnp.where(first_x, 0.0, pltpu.roll(mid[5], 1, 1))
                    diag_here = [low + nxt[0]] + [mid[xi] + nxt[xi + 1] for xi in range(5)]
                    for xi in range(6):
                        below = src[xi, pl.ds(r - 1, 8), :]
                        above = src[xi, pl.ds(r + 1, 8), :]
                        if zt == 0:
                            below = jnp.where(sub == 0, 0.0, below)
                        if zt == 5:
                            above = jnp.where(sub == 7, 0.0, above)
                        beside = (diag_here[xi] + diag_before[xi]) + (below + above)
                        d = diag[xi, pl.ds(dbase + 48 * u + 8 * zt, 8), :]
                        out = (d - root) * mid[xi] + beside
                        dst[xi, pl.ds(r, 8), :] = out
                        if acc is not None:
                            acc[xi] = acc[xi] + out * out
                    if u < UNROLL - 1:
                        diag_before = diag_here[1:] + [mid[5] + past_last(nxt)]
            return None if acc is None else tuple(acc)

        if acc is None:

            @pl.loop(0, B // UNROLL)
            def _(group):
                rows(group, None)

            return None
        return lax.fori_loop(0, B // UNROLL, rows, acc)

    apply(buf_a, buf_b, ROOTS[0], None)
    apply(buf_b, buf_a, ROOTS[1], None)
    apply(buf_a, buf_b, ROOTS[2], None)
    apply(buf_b, buf_a, ROOTS[3], None)
    apply(buf_a, buf_b, ROOTS[4], None)
    sums = apply(buf_b, buf_a, ROOTS[5], (zero,) * 6)
    total = ((sums[0] + sums[1]) + (sums[2] + sums[3])) + (sums[4] + sums[5])

    total = jnp.broadcast_to(jnp.sum(total, axis=0, keepdims=True), (8, LANES))
    for step in (1, 2, 4):
        other = jnp.where(
            lane & step == 0,
            pltpu.roll(total, LANES - step, 1),
            pltpu.roll(total, step, 1),
        )
        total = total + other
    scale = KAPPA * lax.rsqrt(total * (KAPPA * KAPPA / B**3) + 1e-6)
    second = lane >= 64
    count = jnp.where(second, counts[1], counts[0])
    sign = jnp.where(second, signs[1], signs[0]).astype(F32)
    scale = jnp.where((lane // 8) % 8 < count, scale, 0.0)
    weight = (scale * scale * sign)[:1, :]
    scale = scale[:1, :]

    @pl.loop(0, 3)
    def _(c):
        @pl.loop(3 * c, 3 * c + 3)
        def _(pair):
            for h in range(2):
                t = 2 * pair + h
                start = pl.multiple_of(t * LANES, LANES)
                for xi in range(6):
                    field = buf_a[xi, pl.ds(pl.multiple_of(48 + start, 16), LANES), :]
                    filt[xi, pl.ds(start, LANES), :] = (field * scale).astype(BF16)
                    dh, dl = split(field * field * weight)
                    dens = dot(sel[...], jnp.concatenate([dh, dl], 1), NT)
                    box[t + 4, pl.ds(16 + xi, 8, stride=6), :] = dens

        outgoing(c).start()

    shift_x = lax.rem(corners[0, 0], CX)
    lanes_y = lax.rem(corners[0, 1], CY) * B
    whole = lanes_y // LANES
    rest = lax.rem(lanes_y, LANES)
    keep = lane < LANES - rest
    tall = lax.broadcasted_iota(jnp.int32, (16, LANES), 0)
    for j in range(7):
        info = jnp.full((16, LANES), corners[0, 2], jnp.int32)
        for tt in range(3):
            t0 = 3 * j + tt - whole + 4
            vals = []
            for k in range(8):
                rows = pl.ds(16 + 8 * k - shift_x, 8)
                merged = jnp.where(keep, box[t0, rows, :], box[t0 - 1, rows, :])
                vals.append(pltpu.roll(merged, rest, 1))
            top = [jnp.abs(v) for v in vals]
            while len(top) > 1:
                top = [jnp.maximum(top[n], top[n + 1]) for n in range(0, len(top), 2)]
            top = jnp.maximum(jnp.max(top[0], axis=0, keepdims=True), 1e-30)
            power = jnp.ceil(jnp.log2(jnp.broadcast_to(top, (8, LANES))))
            factor = jnp.exp2(BITS - power)
            exponent = jnp.broadcast_to(power[:1, :], (16, LANES)).astype(jnp.int32)
            info = jnp.where(tall == tt, exponent, info)
            for i in range(4):
                code = []
                for v in vals[2 * i : 2 * i + 2]:
                    v = v * factor
                    code.append((v + jnp.where(v < 0, -0.5, 0.5)).astype(jnp.int32))
                code = jnp.concatenate(code, 0).astype(jnp.int16)
                sends[i][j, 16 * tt : 16 * tt + 16, :] = code
        for i in range(4):
            sends[i][j, 48:64, :] = info.astype(jnp.int16)
    for c in range(3):
        outgoing(c).wait()


def filter_and_box(corners, signs, counts, orbitals, potential, eye, sel):
    vm = pl.BlockSpec(memory_space=pltpu.VMEM)
    sm = pl.BlockSpec(memory_space=pltpu.SMEM)
    hbm = pl.BlockSpec(memory_space=pl.ANY)
    return pl.pallas_call(
        cheb_kernel,
        out_shape=[jax.ShapeDtypeStruct((6, YZ, LANES), BF16)]
        + [jax.ShapeDtypeStruct((7, PIECE, LANES), jnp.int16)] * 4,
        in_specs=[sm, sm, sm, hbm, hbm, vm, vm],
        out_specs=[hbm] + [vm] * 4,
        scratch_shapes=[
            pltpu.VMEM((16, B, YZ), BF16),
            pltpu.VMEM((2, B, YZ), F32),
            pltpu.VMEM((6, YZ, LANES), BF16),
            pltpu.VMEM((6, YZ + 96, LANES), F32),
            pltpu.VMEM((6, YZ + 96, LANES), F32),
            pltpu.VMEM((6, YZ, LANES), F32),
            pltpu.VMEM((4, 16 * B, LANES), F32),
            pltpu.VMEM((26, 80, LANES), F32),
            pltpu.SemaphoreType.DMA((2, 3)),
        ],
        compiler_params=pltpu.CompilerParams(vmem_limit_bytes=60 * 1024 * 1024),
        name="cheb",
    )(corners, signs, counts, orbitals, potential, eye, sel)


def natural_kernel(field, eye, out, stages):
    for h in range(3):
        stage = stages.at[h]
        cells = slice(h * LANES, (h + 1) * LANES)
        for xi in range(6):
            turned = dot(eye[...], field[xi, cells, :], NT)
            for fo in range(16):
                stage[pl.ds(fo * B + xi, 8, stride=6), :] = turned[8 * fo : 8 * fo + 8, :]
        for fo in range(16):
            out[fo, :, cells] = stage[fo * B : (fo + 1) * B, :].astype(BF16)


def natural(field, eye):
    return pl.pallas_call(
        natural_kernel,
        grid=(TILES // 3,),
        out_shape=jax.ShapeDtypeStruct((16, B, YZ), BF16),
        in_specs=[
            pl.BlockSpec((6, 3 * LANES, LANES), lambda t: (0, t, 0)),
            pl.BlockSpec((LANES, LANES), lambda t: (0, 0)),
        ],
        out_specs=pl.BlockSpec((16, B, 3 * LANES), lambda t: (0, 0, t)),
        scratch_shapes=[pltpu.VMEM((3, 16 * B, LANES), F32)],
        cost_estimate=pl.CostEstimate(
            flops=2 * 108 * 128**3, bytes_accessed=4 * 16 * B * YZ, transcendentals=0
        ),
        name="natural",
    )(field, eye)


def slot_of(lane):
    return (lane // 16) % 4


def patch_kernel(*refs):
    tab_h, tab_l, dens, out, grid = refs[10:]
    lane = lax.broadcasted_iota(jnp.int32, (8, LANES), 1)
    zero = jnp.zeros((8, LANES), F32)
    for a in range(4):
        for k in range(16):
            grid[a, 8 * k : 8 * k + 8, :] = zero
    pieces = [(u, 0) for u in refs[:4]]
    pieces += [(q, n) for q in refs[4:10] for n in range(4)]
    infos = [ref[n, 48:64, :].astype(jnp.int32) for ref, n in pieces]
    zs = [jnp.max(info[3:4, :]) for info in infos]
    for (ref, n), info, z0 in zip(pieces, infos, zs):
        tiles = []
        for tt in range(3):
            factor = jnp.exp2(info[tt : tt + 1, :].astype(F32) - BITS)
            tiles.append(ref[n, 16 * tt : 16 * tt + 16, :].astype(jnp.int32).astype(F32) * factor)
        a = z0 // LANES
        nxt = lax.rem(a + 1, 4)
        start = lax.rem(z0, LANES)
        stays = lane >= start
        for k in range(2):
            moved = []
            for y in range(8):
                tile, off = (B * y) // LANES, (B * y) % LANES
                v = tiles[tile][8 * k : 8 * k + 8, :]
                if off + B > LANES:
                    v = jnp.where(lane >= off, v, tiles[tile + 1][8 * k : 8 * k + 8, :])
                    window = (lane >= off) | (lane < off + B - LANES)
                else:
                    window = (lane >= off) & (lane < off + B)
                v = jnp.where(window, v, 0.0)
                moved.append(pltpu.roll(v, lax.rem(z0 + (LANES - off), LANES), 1))
            here = [grid[a, y * 16 + 8 * k : y * 16 + 8 * k + 8, :] for y in range(8)]
            there = [grid[nxt, y * 16 + 8 * k : y * 16 + 8 * k + 8, :] for y in range(8)]
            for y in range(8):
                rows = slice(y * 16 + 8 * k, y * 16 + 8 * k + 8)
                grid[a, rows, :] = here[y] + jnp.where(stays, moved[y], 0.0)
                grid[nxt, rows, :] = there[y] + jnp.where(stays, 0.0, moved[y])
    for x in range(16):
        for a in range(4):
            dens[x, :, a * LANES : (a + 1) * LANES] = grid[a, pl.ds(x, 8, stride=16), :]
    rho = jnp.concatenate([grid[a] for a in range(4)], 1)
    rho_h, rho_l = split(rho)
    wide = dot(tab_h[...], jnp.concatenate([rho_h, rho_l], 0), NT)
    spec = wide[:, :LANES] + (wide[:, LANES:] + dot(tab_l[...], rho_h, NT))
    slot = slot_of(lax.broadcasted_iota(jnp.int32, (LANES, LANES), 1))
    for q in range(4):
        final = spec[q * LANES : (q + 1) * LANES, :]
        for m in range(4):
            if m != q:
                part = pltpu.roll(spec[m * LANES : (m + 1) * LANES, :], (16 * (m - q)) % LANES, 1)
                final = jnp.where(slot == m, part, final)
        out[pl.ds(q, LANES, stride=4), :] = final


def patch(pieces, tab_h, tab_l):
    def first(count):
        return pl.BlockSpec((count, PIECE, LANES), lambda i: (0, 0, 0))

    def whole(*shape):
        return pl.BlockSpec(shape, lambda i: (0,) * len(shape))

    return pl.pallas_call(
        patch_kernel,
        grid=(1,),
        out_shape=(
            jax.ShapeDtypeStruct((CX, CY, NZ), F32),
            jax.ShapeDtypeStruct((512, LANES), F32),
        ),
        in_specs=[first(1)] * 4 + [first(4)] * 6 + [whole(512, 512)] * 2,
        out_specs=(whole(CX, CY, NZ), whole(512, LANES)),
        scratch_shapes=[pltpu.VMEM((4, LANES, LANES), F32)],
        name="patch",
    )(*pieces, tab_h, tab_l)


def wave(length, position):
    signed = jnp.where(position <= length // 2, position, position - length)
    k = signed.astype(F32) * (2 * math.pi / length)
    return k * k


def middle_kernel(data, ry, ryt, bx, bxt, out):
    slab = jnp.concatenate([data[r * LANES : (r + 1) * LANES, :] for r in range(4)], 1)
    slab_h, slab_l = split(slab)
    pair = jnp.concatenate([ry[0], ry[0]], 1)
    both = dot(pair, jnp.concatenate([slab_h, slab_l], 0)) + dot(ry[1], slab_h)
    wide = lax.broadcasted_iota(jnp.int32, (1, 512), 1)
    upper = wide % LANES >= 64
    mixed = jnp.where(upper, both[256:], both[:256])
    spec = dot_right(mixed, bx[0], bx[1])
    column = lax.broadcasted_iota(jnp.int32, (1, 256), 1)
    device = lax.axis_index("row") * 32 + lax.axis_index("col")
    kx = wave(NX, column % NX)
    kz = wave(NZ, (column // NX) * LANES + device)
    ky = wave(NY, lax.broadcasted_iota(jnp.int32, (NY, 256), 0))
    k_square = (kx + ky) + kz
    factor = jnp.where(k_square > 0, SCREEN / (k_square + SCREEN), 0.0)
    back = dot_right(spec * factor, bxt[0], bxt[1])
    both = dot_left(ryt[0], ryt[1], back)
    mixed = jnp.where(upper, both[LANES:], both[:LANES])
    for r in range(4):
        out[r * LANES : (r + 1) * LANES, :] = mixed[:, r * LANES : (r + 1) * LANES]


def middle(data, ry, ryt, bx, bxt):
    vm = pl.BlockSpec(memory_space=pltpu.VMEM)
    return pl.pallas_call(
        middle_kernel,
        out_shape=jax.ShapeDtypeStruct((512, LANES), F32),
        in_specs=[vm] * 5,
        out_specs=vm,
        name="middle",
    )(data, ry, ryt, bx, bxt)


def final_kernel(data, tab_h, tab_l, hart, grid):
    slot = slot_of(lax.broadcasted_iota(jnp.int32, (LANES, LANES), 1))
    parts = [data[pl.ds(q, LANES, stride=4), :] for q in range(4)]
    blocks = []
    for m in range(4):
        block = parts[m]
        for q in range(4):
            if q != m:
                block = jnp.where(slot == q, pltpu.roll(parts[q], (16 * (q - m)) % LANES, 1), block)
        blocks.append(block.T)
    spec = jnp.concatenate(blocks, 1)
    field = dot_right(spec, tab_h[...], tab_l[...])
    for a in range(4):
        grid[a] = field[:, a * LANES : (a + 1) * LANES]
    for x in range(16):
        for a in range(4):
            hart[x, :, a * LANES : (a + 1) * LANES] = grid[a, pl.ds(x, 8, stride=16), :]


def final(data, tab_h, tab_l):
    vm = pl.BlockSpec(memory_space=pltpu.VMEM)
    return pl.pallas_call(
        final_kernel,
        out_shape=jax.ShapeDtypeStruct((CX, CY, NZ), F32),
        in_specs=[vm] * 3,
        out_specs=vm,
        scratch_shapes=[pltpu.VMEM((4, LANES, LANES), F32)],
        name="final",
    )(data, tab_h, tab_l)


def real_basis(n):
    index = np.arange(n)
    angle = 2 * np.pi * (np.outer(index, index) % n) / n
    basis = np.where((index <= n // 2)[:, None], np.cos(angle), np.sin(angle)) * np.sqrt(2 / n)
    basis[0] = np.sqrt(1 / n)
    basis[n // 2] = np.where(index % 2 == 0, 1, -1) * np.sqrt(1 / n)
    return basis


def halves(table):
    table = np.ascontiguousarray(table).astype(np.float32)
    high = table.astype(BF16)
    low = (table - high.astype(np.float32)).astype(BF16)
    return high, low


def constants():
    rz = real_basis(NZ)
    ry = real_basis(NY).reshape(NY, 32, 2, 4).transpose(2, 0, 1, 3).reshape(2 * NY, LANES)
    ryt = ry.reshape(2, NY, LANES).transpose(0, 2, 1).reshape(2 * LANES, NY)
    rx = real_basis(NX).reshape(NX, 4, 16)
    bx = np.einsum("krx,mn->rmxnk", rx, np.eye(4))
    bx = np.broadcast_to(bx[:, None], (4, 2, 4, 16, 4, NX)).reshape(512, 256)
    return dict(
        rz=halves(rz),
        ry=np.stack(halves(ry)),
        ryt=np.stack(halves(ryt)),
        bx=np.stack(halves(bx)),
        bxt=np.stack(halves(bx.T)),
        eye=np.eye(LANES).astype(BF16),
        sel=(np.arange(2 * LANES)[None, :] % 8 == np.arange(8)[:, None]).astype(BF16),
    )


def passed_along(value, axis, by):
    peers = lax.axis_size(axis)
    return lax.ppermute(value, axis, [(i, (i + by) % peers) for i in range(peers)])


def shards(orbitals, potential_boxes, corners, signs, counts):
    tab = constants()
    field, *send = filter_and_box(
        corners,
        signs,
        counts,
        orbitals.reshape(16, B, YZ),
        potential_boxes,
        tab["eye"],
        tab["sel"],
    )
    filtered = natural(field, tab["eye"])
    rows = [send[0]] + [passed_along(send[i], "row", i) for i in range(1, 4)]
    got = [
        passed_along(jnp.concatenate([u[j : j + 1] for u in rows]), "col", j) for j in range(1, 7)
    ]
    density, packed = patch((*rows, *got), *tab["rz"])
    packed = lax.all_to_all(packed, BOTH, split_axis=0, concat_axis=0, tiled=True)
    packed = middle(packed, tab["ry"], tab["ryt"], tab["bx"], tab["bxt"])
    packed = lax.all_to_all(packed, BOTH, split_axis=0, concat_axis=0, tiled=True)
    hartree = final(packed, *tab["rz"])
    return (filtered.reshape(2, ORB, B, YZ), density, hartree)


def solution(mesh):
    return jax.shard_map(
        shards,
        mesh=mesh,
        in_specs=(
            P(BOTH, None, None, None),
            P(BOTH, None, None),
            P(BOTH, None),
            P(BOTH),
            P(BOTH),
        ),
        out_specs=(
            P(BOTH, None, None, None),
            P("row", "col", None),
            P("row", "col", None),
        ),
        check_vma=False,
    )
```
